512 devices in a mesh: row: 16 (over y, x_lo), col: 32 (over z, x_hi, core).
Axes of the slice: x: 4 (x_hi: 2, x_lo: 2; x = x_hi * 2 + x_lo), y: 8, z: 8, core: 2. Of those that a mesh axis runs over, the one named last changes fastest.
Arguments:
- features: bfloat16 [65536, 128], P(('col', 'row')), may hold values from -6 to 6
- block_ids: int32 [16, 32, 32], P('row', 'col'), may hold values from 0 to 511
- block_values: bfloat16 [16, 32, 32, 128, 128], P('row', 'col'), as said below
- block_count: int32 [16, 32], P('row', 'col'), may hold values from 8 to 32, as said below
- labels: int32 [65536], P(('col', 'row')), may hold values from 0 to 171
- w_first: bfloat16 [128, 512], replicated, may hold values from -0.5 to 0.5
- w_second: bfloat16 [512, 172], replicated, may hold values from -0.25 to 0.25
Outputs:
- logits: float32 [65536, 172], P(('col', 'row'))
- grad_first: float32 [128, 512], replicated
- grad_second: float32 [512, 172], replicated
The draws below stay inside these ranges and needn't reach their ends.
Inputs may be any that keep to these rules, and one draw needn't show every extreme that they name: Only the first block_count slots of a tile are blocks of the graph; every tile has at least a quarter of its 32 slots live, and some tile has all of them. `block_ids`: A position may be listed more than once in a tile. `block_values`: entries are nonnegative.
All inputs are finite; a program needn't handle non-finite values.
Results may differ from the reference program's by a relative error of at most 0.0033.
Values may be sent and summed in bfloat16 or wider, within the bound.
A program may use at most 64 MiB of HBM per device.

```python
import math
import jax
import jax.numpy as jnp
import numpy as np
from jax import lax

F0 = 128
HID = 512
K = 172
BLOCK = 128
NODES_DEV = 128
NBLK = 32
NODES = 65536
RB = 32
CB = 16
N_ROW = 16
N_COL = 32


def draw_block_count(key, part):
    divisor = jax.random.randint(key, (N_ROW, N_COL), 1, 5)
    counts = NBLK // divisor
    chosen = jax.random.randint(jax.random.fold_in(key, 7), (), 0, N_ROW * N_COL)
    flat = jnp.arange(N_ROW * N_COL).reshape(N_ROW, N_COL)
    return jnp.where(flat == chosen, NBLK, counts).astype(jnp.int32)


def draw_block_values(key, part):
    upper = (3.0 * NODES_DEV / (NBLK * 8192)) ** 0.5
    base = jax.random.uniform(key, (N_ROW, N_COL, NBLK, BLOCK, BLOCK), jnp.float32, 0.0, upper)
    exponents = jax.random.uniform(jax.random.fold_in(key, 11), (N_ROW,), jnp.float32, 0.0, math.log(10.0))
    chosen = jax.random.randint(jax.random.fold_in(key, 13), (), 0, N_ROW)
    exponents = jnp.where(jnp.arange(N_ROW) == chosen, math.log(10.0), exponents)
    factor = jnp.exp(exponents) / 4.64
    return (base * factor[:, None, None, None, None]).astype(jnp.bfloat16)


def place_ends(values, key, least, high):
    dims = values.shape
    place = [jax.random.randint(jax.random.fold_in(key, axis), (), 0, dims[axis]) for axis in range(len(dims))]
    values = values.at[tuple(place)].set(least)
    longest = dims.index(max(dims))
    place[longest] = (place[longest] + 1) % dims[longest]
    return values.at[tuple(place)].set(high)


def shard_levels(own_key, extent, shards, least, high):
    gain, own = 1.0, jax.random.fold_in(own_key, 6)
    for position, parts in shards:
        draws = jnp.exp(jax.random.uniform(jax.random.fold_in(own, position), (parts,), jnp.float32, least / len(shards), high / len(shards)))
        gain = gain * jnp.repeat(draws, extent[position] // parts).reshape([-1 if axis == position else 1 for axis in range(len(extent))])
    return gain


def rank_bounds(count, skew):
    weights = [(1 << 20) // math.isqrt(rank ** skew) + 1 for rank in range(1, count + 1)]
    scale = 1 + sum(weights) // (1 << 30)
    return np.cumsum(np.array([max(1, weight // scale) for weight in weights]))


def ranked_ids(own_key, dims, number_of, skew):
    listing = rank_bounds(number_of, skew)
    ticket = jax.random.randint(jax.random.fold_in(own_key, 1), dims, 0, int(listing[number_of - 1]))
    grade = jnp.searchsorted(jnp.asarray(listing, jnp.int32), ticket, side="right")
    return jax.random.permutation(jax.random.fold_in(own_key, 2), number_of)[grade].astype(jnp.int32)


def noise(rng, extent, scale, bound, split=(), held_as=jnp.bfloat16):
    loudness = shard_levels(rng, extent, split, -0.22, 0.18) if split else 1.0
    drawn = jax.random.normal(rng, extent, jnp.float32) * scale * loudness
    return jnp.minimum(jnp.maximum(drawn, -bound), bound).astype(held_as)


def setup_inputs(seed: int = 0) -> dict:
    arg_keys = jax.random.split(jax.random.key(seed), 8)
    return {
        "features": noise(arg_keys[0], (NODES, F0), 1.0, 6.0, ((0, 512),)),
        "block_ids": place_ends(ranked_ids(arg_keys[1], (N_ROW, N_COL, NBLK), RB * CB, 2), jax.random.fold_in(arg_keys[1], 3), 0, (RB * CB) - 1).astype(jnp.int32),
        "block_values": draw_block_values(jax.random.fold_in(arg_keys[7], 71), 0),
        "block_count": draw_block_count(jax.random.fold_in(arg_keys[7], 71), 0),
        "labels": place_ends(jax.random.randint(arg_keys[4], (NODES,), 0, K), jax.random.fold_in(arg_keys[4], 1), 0, K - 1).astype(jnp.int32),
        "w_first": noise(arg_keys[5], (F0, HID), F0 ** -0.5, 0.5),
        "w_second": noise(arg_keys[6], (HID, K), HID ** -0.5, 0.25),
    }


def live_values(values, live_count):
    alive = jnp.arange(NBLK) < live_count
    return jnp.where(alive[:, None, None], values.astype(jnp.float32), jnp.zeros((), jnp.float32))


def forward_term(values, block_ids, live_count, panel):
    picked = panel[block_ids % CB]
    products = jnp.einsum('bij,bjf->bif', live_values(values, live_count), picked.astype(jnp.float32))
    summed = jax.ops.segment_sum(products, block_ids // CB, num_segments=RB)
    return summed.reshape(RB * BLOCK, panel.shape[-1])


def reverse_term(values, block_ids, live_count, panel):
    picked = panel[block_ids // CB]
    products = jnp.einsum('bji,bjf->bif', live_values(values, live_count), picked.astype(jnp.float32))
    summed = jax.ops.segment_sum(products, block_ids % CB, num_segments=CB)
    return summed.reshape(CB * BLOCK, panel.shape[-1])


def aggregate_rows(block_ids, block_values, block_count, panels):
    width = panels.shape[-1]

    def one_row(row_index):
        def add(total, col_index):
            term = forward_term(block_values[row_index, col_index], block_ids[row_index, col_index],
                                block_count[row_index, col_index], panels[col_index])
            return total + term, None

        total, _ = lax.scan(add, jnp.zeros((RB * BLOCK, width), jnp.float32), jnp.arange(N_COL))
        return total

    return lax.map(one_row, jnp.arange(N_ROW)).reshape(NODES, width)


def aggregate_cols(block_ids, block_values, block_count, panels):
    width = panels.shape[-1]

    def one_col(col_index):
        def add(total, row_index):
            term = reverse_term(block_values[row_index, col_index], block_ids[row_index, col_index],
                                block_count[row_index, col_index], panels[row_index])
            return total + term, None

        total, _ = lax.scan(add, jnp.zeros((CB * BLOCK, width), jnp.float32), jnp.arange(N_ROW))
        return total

    return lax.map(one_col, jnp.arange(N_COL)).reshape(NODES, width)


def reference(features, block_ids, block_values, block_count, labels, w_first, w_second):
    agg_first = aggregate_rows(block_ids, block_values, block_count,
                               features.reshape(N_COL, CB, BLOCK, F0)).astype(jnp.bfloat16)
    pre_first = jnp.dot(agg_first, w_first, preferred_element_type=jnp.float32)
    hidden = jnp.maximum(pre_first, 0.0).astype(jnp.bfloat16)
    second_in = jnp.dot(hidden, w_second, preferred_element_type=jnp.float32).astype(jnp.bfloat16)
    logits = aggregate_cols(block_ids, block_values, block_count, second_in.reshape(N_ROW, RB, BLOCK, K))
    top = jnp.max(logits, axis=1, keepdims=True)
    expo = jnp.exp(logits - top)
    prob = expo / jnp.sum(expo, axis=1, keepdims=True)
    onehot = (labels[:, None] == jnp.arange(K, dtype=jnp.int32)[None, :]).astype(jnp.float32)
    d_logits = (prob - onehot).astype(jnp.bfloat16)
    d_second = aggregate_rows(block_ids, block_values, block_count,
                              d_logits.reshape(N_COL, CB, BLOCK, K)).astype(jnp.bfloat16)
    d_hidden = jnp.dot(d_second, w_second.T, preferred_element_type=jnp.float32)
    d_pre = jnp.where(pre_first > 0.0, d_hidden, jnp.zeros_like(d_hidden)).astype(jnp.bfloat16)
    grad_first = jnp.dot(agg_first.T, d_pre, preferred_element_type=jnp.float32)
    grad_second = jnp.dot(hidden.T, d_second, preferred_element_type=jnp.float32)
    return logits, grad_first, grad_second
```

```python
import jax
import jax.numpy as jnp
from jax import lax
from jax.experimental import pallas as pl
from jax.experimental.pallas import tpu as pltpu
from jax.sharding import PartitionSpec as P

MESH = pl.DeviceIdType.MESH
BLOCK = 128
CLASSES = 172
WIDE = 176
OFFSETS = (4, 3, 5, 2, 6, 1, 7)
NEAR = tuple(reversed(range(7)))
F32 = jnp.float32
BF16 = jnp.bfloat16
VM = pl.BlockSpec(memory_space=pltpu.VMEM)
SM = pl.BlockSpec(memory_space=pltpu.SMEM)
ANY = pl.BlockSpec(memory_space=pl.ANY)
DMA = pltpu.SemaphoreType.DMA


class Place:
    def __init__(self):
        self.row = lax.axis_index("row")
        self.col = lax.axis_index("col")
        self.y = self.row // 2
        self.xl = self.row % 2
        self.z = self.col // 4
        self.xh = (self.col // 2) % 2
        self.core = self.col % 2

    def along_y(self, offset):
        return (self.y + offset) % 8

    def along_z(self, offset):
        return (self.z + offset) % 8

    def y_peer(self, offset):
        return (self.along_y(offset) * 2 + self.xl, self.col)

    def z_peer(self, offset):
        return (self.row, self.along_z(offset) * 4 + self.xh * 2 + self.core)

    def lo_peer(self):
        return (self.y * 2 + 1 - self.xl, self.col)

    def hi_peer(self):
        return (self.row, self.z * 4 + (1 - self.xh) * 2 + self.core)

    def twin(self):
        return (self.row, self.z * 4 + self.xh * 2 + 1 - self.core)

    def row_peer(self, offset):
        return ((self.row + offset) % 16, self.col)

    def half(self):
        return self.z * 2 + self.xh

    def half_peer(self, offset):
        return (self.row, ((self.half() + offset) % 16) * 2 + self.core)


def send(src, dst, send_sem, recv_sem, peer):
    copy = pltpu.make_async_remote_copy(
        src_ref=src, dst_ref=dst, send_sem=send_sem, recv_sem=recv_sem, device_id=peer, device_id_type=MESH
    )
    copy.start()
    return copy


def greet(peers):
    barrier = pltpu.get_barrier_semaphore()
    for peer in peers:
        pl.semaphore_signal(barrier, inc=1, device_id=peer, device_id_type=MESH)
    pl.semaphore_wait(barrier, len(peers))


def gather_row(me, own, panel, y_send, y_recv, x_send, x_recv, work=None):
    index = me.row
    first = send(own, panel.at[index], x_send.at[7], x_recv.at[7], me.lo_peer())
    along = [None] * 7
    for i in NEAR:
        along[i] = send(own, panel.at[index], y_send.at[i], y_recv.at[i], me.y_peer(OFFSETS[i]))
    local = pltpu.make_async_copy(own, panel.at[index], y_send.at[7])
    local.start()
    if work is not None:
        work()
    across = [first]
    for i in NEAR:
        along[i].wait_recv()
        source = me.along_y(8 - OFFSETS[i]) * 2 + me.xl
        across.append(send(panel.at[source], panel.at[source], x_send.at[i], x_recv.at[i], me.lo_peer()))
    local.wait()
    for copy in across:
        copy.wait_recv()
    return along + across


def encode(value, ref, index):
    near = (jnp.sum(value, axis=0, keepdims=True) * (1.0 / BLOCK)).astype(BF16)
    ref[index, :BLOCK, :] = (value - near.astype(F32)).astype(BF16)
    ref[index, BLOCK:, :] = jnp.broadcast_to(near, (16, BLOCK))


def decode(ref, index):
    return ref[index, :BLOCK, :].astype(F32) + ref[index, BLOCK:, :].astype(F32)[:1]


def sum_by_slot(table, links, acc, product):
    def multiply(s, carry):
        acc[s + 1] = product(s)
        return carry

    lax.fori_loop(0, 32, multiply, 0, unroll=8)

    def chain(s, carry):
        acc[s + 1] = acc[s + 1] + acc[table[links, s]]
        return carry

    lax.fori_loop(0, 32, chain, 0, unroll=4)


def reduce_all(me, a_in, b_in, a_out, b_out, a_twin, b_twin, a_half, b_half, a_cut, b_cut, a_got, b_got, a_all, b_all,
               send_sem, recv_sem):
    lanes = ((a_in, a_out, a_twin, a_half, a_cut, a_got, a_all, 24, me.row_peer, me.row, me.half_peer, me.half()),
             (b_in, b_out, b_twin, b_half, b_cut, b_got, b_all, 16, me.half_peer, me.half(), me.row_peer, me.row))

    def rows(index, size):
        return pl.ds(pl.multiple_of(index * size, 8), size)

    def settle(ref, stage, which):
        return pltpu.make_async_remote_copy(
            src_ref=ref, dst_ref=ref, send_sem=send_sem.at[stage, which], recv_sem=recv_sem.at[stage, which],
            device_id=me.twin(), device_id_type=MESH)

    swaps = []
    for which, (source, out, twin, half, cut, got, every, size, peer1, at1, peer2, at2) in enumerate(lanes):
        swaps.append(send(source.at[rows(1 - me.core, 16 * size)], twin, send_sem.at[0, which], recv_sem.at[0, which], me.twin()))
    for which, (source, out, twin, half, cut, got, every, size, peer1, at1, peer2, at2) in enumerate(lanes):
        swaps[which].wait_recv()
        half[...] = source[rows(me.core, 16 * size), :] + twin[...]
        for k in range(16):
            cut[k] = half[k * size:(k + 1) * size, :].astype(BF16)
        for k in range(1, 16):
            send(cut.at[(at1 + k) % 16], got.at[k - 1], send_sem.at[1, which], recv_sem.at[1, which], peer1(k))
    for which, (source, out, twin, half, cut, got, every, size, peer1, at1, peer2, at2) in enumerate(lanes):
        settle(got, 1, which).wait_recv()
        total = half[rows(at1, size), :]
        for k in range(15):
            total = total + got[k].astype(F32)
        every[at2] = total.astype(BF16)
        for k in range(1, 16):
            send(every.at[at2], every.at[at2], send_sem.at[2, which], recv_sem.at[2, which], peer2(k))
    for which, (source, out, twin, half, cut, got, every, size, peer1, at1, peer2, at2) in enumerate(lanes):
        settle(got, 2, which).wait_recv()
        total = every[0].astype(F32)
        for k in range(1, 16):
            total = total + every[k].astype(F32)
        place = rows(me.core * 16 + at1, size)
        out[place, :] = total
        for k in range(1, 16):
            send(out.at[place], out.at[place], send_sem.at[3, which], recv_sem.at[3, which], peer1(k))
    last = []
    for which, (source, out, twin, half, cut, got, every, size, peer1, at1, peer2, at2) in enumerate(lanes):
        settle(out.at[pl.ds(0, 15 * size)], 3, which).wait_recv()
        part = out.at[rows(me.core, 16 * size)]
        last.append(send(part, part, send_sem.at[4, which], recv_sem.at[4, which], me.twin()))
    for copy in last:
        copy.wait_recv()
    for which, (source, out, twin, half, cut, got, every, size, peer1, at1, peer2, at2) in enumerate(lanes):
        swaps[which].wait_send()
        settle(got, 1, which).wait_send()
        settle(got, 2, which).wait_send()
        settle(out.at[pl.ds(0, 15 * size)], 3, which).wait_send()
        last[which].wait_send()


def link_tables(ids, ids_wide, count, rows, table_v, table_s, sem):
    rows[...] = jnp.zeros_like(rows)
    rows[0:1, 0:32] = ids_wide[...]
    every = rows[0:1, :]
    lane = lax.broadcasted_iota(jnp.int32, (1, BLOCK), 1)
    none = jnp.zeros((1, BLOCK), jnp.int32)

    def row_place(x):
        r = x // 16
        return (r % 2) * 16 + ((r // 2) % 2) * 8 + r // 4

    def col_place(x):
        return (x % 2) * 8 + (x % 16) // 2

    row_every, col_every = row_place(every), col_place(every)

    def add(t, carry):
        row_before, row_last, col_before, col_last = carry
        row, col = row_place(ids[0, t]), col_place(ids[0, t])
        late = (lane > t) & (t < count)
        alive = (lane >= 0) & (t < count)
        return (jnp.where(late & (row_every == row), t + 1, row_before), jnp.where(alive & (lane == row), t + 1, row_last),
                jnp.where(late & (col_every == col), t + 1, col_before), jnp.where(alive & (lane == col), t + 1, col_last))

    row_before, row_last, col_before, col_last = lax.fori_loop(0, 32, add, (none, none, none, none))
    for at, line in enumerate((every % 16, row_before, row_last, row_every, col_before, col_last)):
        table_v[at:at + 1, :] = line
    copy = pltpu.make_async_copy(table_v, table_s, sem)
    copy.start()
    return copy


def everything(features, ids, ids_wide, count, values_any, labels, w1_any, w2_in, logits_t, b_out, a_out,
               rows, table_v, table, values, w1, w2, panel, acc, part, from_twin, to_hi, from_hi, to_z, from_z, agg,
               hidden, second, acc_wide, to_x, from_x, to_y, from_y, grads, panel_wide, grad,
               acc_first, acc_second, a_in, b_in, a_twin, b_twin, a_half, b_half, a_cut, b_cut, a_got, b_got, a_all, b_all,
               load, fs_y, fr_y, fs_x, fr_x, c_send, c_recv, h_send, h_recv, z_send, z_recv,
               ac_send, ac_recv, ah_send, ah_recv, az_send, az_recv, x_send, x_recv, y_send, y_recv,
               ax_send, ax_recv, ay_send, ay_recv, send_sem, recv_sem):
    me = Place()
    barrier = pltpu.get_barrier_semaphore()
    peers = [me.twin()] + [me.row_peer(k) for k in range(1, 16)] + [me.half_peer(k) for k in range(1, 16)]
    for peer in peers:
        pl.semaphore_signal(barrier, inc=1, device_id=peer, device_id_type=MESH)
    loads = [pltpu.make_async_copy(src, dst, load.at[i]) for i, (src, dst) in
             enumerate(((values_any.at[0, 0], values), (w1_any, w1)))]
    for copy in loads:
        copy.start()
    tabled = link_tables(ids, ids_wide, count[0, 0], rows, table_v, table, load.at[3])
    w2[...] = jnp.zeros_like(w2)
    w2[:CLASSES, :] = w2_in[...]
    acc[0] = jnp.zeros(acc.shape[1:], F32)
    acc_wide[0] = jnp.zeros(acc_wide.shape[1:], F32)
    pl.semaphore_wait(barrier, len(peers))
    sent = []
    sent += gather_row(me, features, panel, fs_y, fr_y, fs_x, fr_x)
    for copy in loads:
        copy.wait()
    tabled.wait()

    sum_by_slot(table, 1, acc, lambda s: jnp.dot(values[s], panel[table[0, s]], preferred_element_type=F32))
    mine, theirs = me.core * 16, (1 - me.core) * 16
    near, far = me.xh * 8, (1 - me.xh) * 8

    def partial(at):
        return acc[table[2, at]]

    halves = []
    for k, side in enumerate((far, near)):
        for q in range(8):
            part[k * 8 + q] = partial(theirs + side + q)
        halves.append(send(part.at[pl.ds(k * 8, 8)], from_twin.at[pl.ds(side, 8)], c_send.at[k], c_recv.at[k], me.twin()))
    halves[0].wait_recv()
    hops = []
    for i, step in enumerate(OFFSETS + (0,)):
        at = me.along_z(step)
        encode(partial(mine + far + at) + from_twin[far + at], to_hi, at)
        hops.append(send(to_hi.at[at], from_hi.at[at], h_send.at[i], h_recv.at[i], me.hi_peer()))
    halves[1].wait_recv()
    rounds = []
    for i, step in enumerate(OFFSETS):
        at = me.along_z(step)
        hops[i].wait_recv()
        encode(partial(mine + near + at) + from_twin[near + at] + decode(from_hi, at), to_z, at)
        rounds.append(send(to_z.at[at], from_z.at[i], z_send.at[i], z_recv.at[i], me.z_peer(step)))
    hops[7].wait_recv()
    total = partial(mine + near + me.z) + from_twin[near + me.z] + decode(from_hi, me.z)
    for i in range(7):
        rounds[i].wait_recv()
        total = total + decode(from_z, i)
    own = mine + near + me.z
    agg[own] = total.astype(BF16)
    sent += halves + hops + rounds

    def dense(places):
        pre = jnp.dot(jnp.concatenate([agg[at] for at in places], axis=0), w1[...], preferred_element_type=F32)
        kept = jnp.maximum(pre, 0.0).astype(BF16)
        turned = lax.dot_general(w2[...], kept, (((1,), (1,)), ((), ())), preferred_element_type=F32).astype(BF16)
        for k, at in enumerate(places):
            hidden[at] = kept[k * BLOCK:(k + 1) * BLOCK]
            second[at] = turned[:, k * BLOCK:(k + 1) * BLOCK]

    block = agg.at[own]
    across = [None] * 8
    along = [None] * 7
    twins = [None] * 16
    across[7] = send(block, block, ah_send.at[7], ah_recv.at[7], me.hi_peer())
    for i in NEAR:
        along[i] = send(block, block, az_send.at[i], az_recv.at[i], me.z_peer(OFFSETS[i]))
    twins[15] = send(block, block, ac_send.at[15], ac_recv.at[15], me.twin())
    across[7].wait_recv()
    other = mine + far + me.z
    twins[14] = send(agg.at[other], agg.at[other], ac_send.at[14], ac_recv.at[14], me.twin())
    ready = [own, other]
    late = [(15, theirs + near + me.z), (14, theirs + far + me.z)]
    for step in (((0, 6), (0, 5)), ((0, 4), (0, 3)), ((1, 6), (1, 5)), ((0, 2), (0, 1)), ((1, 4), (1, 3)), ((0, 0), (1, 2)),
                 ((1, 1), (1, 0)), ()):
        for over_x, i in step:
            source = me.along_z(8 - OFFSETS[i])
            if over_x:
                across[i].wait_recv()
                at = mine + far + source
                twins[7 + i] = send(agg.at[at], agg.at[at], ac_send.at[7 + i], ac_recv.at[7 + i], me.twin())
                late.append((7 + i, theirs + far + source))
            else:
                along[i].wait_recv()
                at = mine + near + source
                across[i] = send(agg.at[at], agg.at[at], ah_send.at[i], ah_recv.at[i], me.hi_peer())
                twins[i] = send(agg.at[at], agg.at[at], ac_send.at[i], ac_recv.at[i], me.twin())
                late.append((i, theirs + near + source))
            ready.append(at)
        while len(ready) < 4:
            k, at = late.pop(0)
            twins[k].wait_recv()
            ready.append(at)
        dense(ready)
        ready = []
    sent += along + across + twins

    sum_by_slot(table, 4, acc_wide, lambda s: jnp.dot(second[table[3, s]], values[s], preferred_element_type=F32))
    mine, theirs = me.xl * 8, (1 - me.xl) * 8

    def scores(at):
        return acc_wide[table[5, at]]

    hops = []
    for i, step in enumerate(OFFSETS + (0,)):
        at = me.along_y(step)
        to_x[at] = scores(theirs + at).astype(BF16)
        hops.append(send(to_x.at[at], from_x.at[at], x_send.at[i], x_recv.at[i], me.lo_peer()))
    rounds = []
    for i, step in enumerate(OFFSETS):
        at = me.along_y(step)
        hops[i].wait_recv()
        to_y[at] = (scores(mine + at) + from_x[at].astype(F32)).astype(BF16)
        rounds.append(send(to_y.at[at], from_y.at[i], y_send.at[i], y_recv.at[i], me.y_peer(step)))
    hops[7].wait_recv()
    total = scores(mine + me.y) + from_x[me.y].astype(F32)
    for i in range(7):
        rounds[i].wait_recv()
        total = total + from_y[i].astype(F32)
    sent += hops + rounds
    kind = lax.broadcasted_iota(jnp.int32, (WIDE, BLOCK), 0)
    live = kind < CLASSES
    shown = jnp.where(live, total, -jnp.inf)
    top = jnp.max(shown, axis=0, keepdims=True)
    expo = jnp.where(live, jnp.exp(shown - top), 0.0)
    norm = jnp.sum(expo, axis=0, keepdims=True)
    grads[...] = (expo / norm - (kind == labels[...]).astype(F32)).astype(BF16)

    def write_logits():
        logits_t[...] = total[:CLASSES]

    sent += gather_row(me, grads, panel_wide, ay_send, ay_recv, ax_send, ax_recv, write_logits)

    sum_by_slot(table, 1, acc_wide, lambda s: lax.dot_general(
        panel_wide[table[0, s]], values[s], (((1,), (1,)), ((), ())), preferred_element_type=F32))
    acc_first[...] = jnp.zeros_like(acc_first)
    acc_second[...] = jnp.zeros_like(acc_second)

    def backward(i, carry):
        for k in range(4):
            grad[:, k * BLOCK:(k + 1) * BLOCK] = acc_wide[table[2, i * 4 + k]].astype(BF16)
        at = pl.ds(i * 4, 4)
        kept = hidden[at].reshape(512, 512)
        back_in = grad[...]
        back = lax.dot_general(back_in, w2[...], (((0,), (0,)), ((), ())), preferred_element_type=F32)
        pre = jnp.where(kept.astype(F32) > 0.0, back, 0.0).astype(BF16)
        acc_first[...] += lax.dot_general(agg[at].reshape(512, 128), pre, (((0,), (0,)), ((), ())), preferred_element_type=F32)
        acc_second[...] += jnp.dot(back_in, kept, preferred_element_type=F32)
        return carry

    lax.fori_loop(0, 8, backward, 0)
    for q in range(4):
        b_in[q * BLOCK:(q + 1) * BLOCK, :] = acc_first[:, q * BLOCK:(q + 1) * BLOCK]
        a_in[q * 192:q * 192 + WIDE, :] = acc_second[:, q * BLOCK:(q + 1) * BLOCK]
        a_in[q * 192 + WIDE:(q + 1) * 192, :] = jnp.zeros((16, BLOCK), F32)
    reduce_all(me, a_in, b_in, a_out, b_out, a_twin, b_twin, a_half, b_half, a_cut, b_cut, a_got, b_got, a_all, b_all,
               send_sem, recv_sem)
    for copy in sent:
        copy.wait_send()


def finish(logits_in, b_out, a_out, logits_t, first_out, second_out):
    logits_t[...] = logits_in[...]
    for q in range(4):
        first_out[:, q * BLOCK:(q + 1) * BLOCK] = b_out[q * BLOCK:(q + 1) * BLOCK, :]
        second_out[:, q * BLOCK:(q + 1) * BLOCK] = a_out[q * 192:q * 192 + CLASSES, :]


def vm(*dims, dtype=BF16):
    return pltpu.VMEM(dims, dtype)


def shards(features, block_ids, block_values, block_count, labels, w_first, w_second):
    scratch = [
        vm(8, 128, dtype=jnp.int32), vm(8, 128, dtype=jnp.int32), pltpu.SMEM((8, 128), jnp.int32),
        vm(32, 128, 128), vm(128, 512), vm(WIDE, 512), vm(16, 128, 128), vm(33, 128, 128, dtype=F32),
        vm(16, 128, 128, dtype=F32), vm(16, 128, 128, dtype=F32), vm(8, 144, 128), vm(8, 144, 128), vm(8, 144, 128),
        vm(7, 144, 128), vm(32, 128, 128), vm(32, 128, 512), vm(32, WIDE, 128), vm(33, WIDE, 128, dtype=F32),
        vm(8, WIDE, 128), vm(8, WIDE, 128), vm(8, WIDE, 128), vm(7, WIDE, 128), vm(WIDE, 128),
        vm(16, WIDE, 128), vm(WIDE, 512), vm(128, 512, dtype=F32), vm(WIDE, 512, dtype=F32),
        vm(768, 128, dtype=F32), vm(512, 128, dtype=F32),
        vm(384, 128, dtype=F32), vm(256, 128, dtype=F32), vm(384, 128, dtype=F32), vm(256, 128, dtype=F32),
        vm(16, 24, 128), vm(16, 16, 128), vm(15, 24, 128), vm(15, 16, 128), vm(16, 24, 128), vm(16, 16, 128),
        DMA((4,)), DMA((8,)), DMA((7,)), DMA((8,)), DMA((8,)), DMA((2,)), DMA((2,)), DMA((8,)), DMA((8,)), DMA((7,)), DMA((7,)),
        DMA((16,)), DMA((16,)), DMA((8,)), DMA((8,)), DMA((7,)), DMA((7,)), DMA((8,)), DMA((8,)), DMA((7,)), DMA((7,)),
        DMA((8,)), DMA((8,)), DMA((8,)), DMA((7,)), DMA((5, 2)), DMA((5, 2)),
    ]
    parts = pl.pallas_call(
        everything,
        out_shape=(jax.ShapeDtypeStruct((CLASSES, 128), F32), jax.ShapeDtypeStruct((512, 128), F32),
                   jax.ShapeDtypeStruct((768, 128), F32)),
        in_specs=[ANY, SM, VM, SM, ANY, VM, ANY, VM],
        out_specs=(VM, VM, VM),
        scratch_shapes=scratch,
        compiler_params=pltpu.CompilerParams(vmem_limit_bytes=60 * 1024 * 1024, collective_id=0, has_side_effects=True),
        name="everything",
    )(features, block_ids[0], block_ids[0], block_count, block_values, labels[None], w_first, w_second.T)
    logits_t, grad_first, second_t = pl.pallas_call(
        finish,
        out_shape=(jax.ShapeDtypeStruct((CLASSES, 128), F32), jax.ShapeDtypeStruct((128, 512), F32),
                   jax.ShapeDtypeStruct((CLASSES, 512), F32)),
        in_specs=[VM, VM, VM],
        out_specs=(VM, VM, VM),
        name="finish",
    )(*parts)
    return logits_t.T, grad_first, second_t.T


def solution(mesh):
    in_specs = (
        P(("col", "row"), None),
        P("row", "col", None),
        P("row", "col", None, None, None),
        P("row", "col"),
        P(("col", "row")),
        P(),
        P(),
    )
    out_specs = (P(("col", "row"), None), P(), P())
    return jax.shard_map(shards, mesh=mesh, in_specs=in_specs, out_specs=out_specs, check_vma=False)
```
